32 devices in a mesh: expert: 16 (over z, y, x), seq: 2 (over core).
Axes of the slice: x: 2, y: 2, z: 4, core: 2. Of those that a mesh axis runs over, the one named last changes fastest.
Arguments:
- out_grad: bfloat16 [4096, 7168], P(('expert', 'seq')), may hold values from -6 to 6
- route_ids: int32 [4096, 8], P('expert'), may hold values from 0 to 255, all different within a row
- route_weights: float32 [4096, 8], P('expert'), may hold values from 0.2 to 1
- gate_pre: bfloat16 [16, 192, 1024], P('expert', None, 'seq'), may hold values from -5 to 5
- up_pre: bfloat16 [16, 192, 1024], P('expert', None, 'seq'), may hold values from -5 to 5
- w_gate: bfloat16 [16, 7168, 1024], P('expert', None, 'seq'), may hold values from -0.75 to 0.75
- w_up: bfloat16 [16, 7168, 1024], P('expert', None, 'seq'), may hold values from -0.75 to 0.75
- w_down: bfloat16 [16, 1024, 7168], P('expert', 'seq'), may hold values from -0.0078125 to 0.0078125
Outputs:
- in_grad: bfloat16 [4096, 7168], P(('expert', 'seq'))
- weight_grad: bfloat16 [4096, 8], P(('expert', 'seq'))
The draws below stay inside these ranges and needn't reach their ends.
Inputs may be any that keep to these rules, and one draw needn't show every extreme that they name: `route_ids`: each row names 8 different experts; only experts below 16 are held in this window, the others are left to other windows.
All inputs are finite; a program needn't handle non-finite values.
Results may differ from the reference program's by a relative error of at most 0.0065.
Values may be sent and summed in bfloat16 or wider, within the bound.
A program may use at most 192 MiB of HBM per device.

```python
import jax
import jax.numpy as jnp
from jax import lax

D = 7168
ROUTED = 256
TOPK = 8
FF = 1024
TOK_DEV = 128
EXPERTS = 16
TOKENS = 4096
CAP = 12
SLOTS = 192
N_EXPERT = 16
N_SEQ = 2


def block_scale(rng, shape, split, low, top_value):
    def one(dim, shards_of):
        steps = jax.random.uniform(jax.random.fold_in(jax.random.fold_in(rng, 6), dim), (shards_of,), jnp.float32, low / len(split), top_value / len(split))
        return jnp.repeat(jnp.exp(steps), shape[dim] // shards_of).reshape((-1,) + (1,) * (len(shape) - dim - 1))

    factor_of = one(*split[0])
    for cut in split[1:]:
        factor_of = factor_of * one(*cut)
    return factor_of


def choose_distinct(rng, rows, amount, top, lift):
    order = jax.random.permutation(jax.random.fold_in(rng, 1), amount)
    pull = order
    for power in range(3):
        pull = pull * pull // amount
    pull = pull * lift // amount
    lots = jax.random.randint(jax.random.fold_in(rng, 2), (rows, amount), 0, 4096) + pull
    sure = jax.random.permutation(jax.random.fold_in(rng, 3), rows)[jnp.arange(amount) % rows]
    lots = jnp.where(jnp.arange(rows)[:, None] == sure[None, :], 1 << 14, lots)
    priority = lots * amount + jnp.arange(amount)
    return lax.top_k(priority.astype(jnp.int32), top)[1].astype(jnp.int32)


def centred(key, dims, spread, reach, shards=(), kind=jnp.bfloat16):
    result = jax.random.normal(key, dims, jnp.float32) * spread
    if len(shards) > 0:
        result = block_scale(key, dims, shards, -0.22, 0.18) * result
    return jnp.clip(result, min=-reach, max=reach).astype(kind)


def setup_inputs(seed: int = 0) -> dict:
    splits = jax.random.split(jax.random.key(seed), 9)
    return {
        "out_grad": centred(splits[0], (TOKENS, D), 1.0, 6.0, ((0, 32),)),
        "route_ids": choose_distinct(splits[1], TOKENS, ROUTED, TOPK, 512),
        "route_weights": jnp.clip(0.2 + 0.8 * jax.random.uniform(splits[2], (TOKENS, TOPK), jnp.float32) ** block_scale(splits[2], (TOKENS, TOPK), ((0, 16),), -0.2, 0.2), 0.2, 1.0),
        "gate_pre": centred(splits[3], (EXPERTS, SLOTS, FF), 1.0, 5.0, ((0, 16), (2, 2))),
        "up_pre": centred(splits[4], (EXPERTS, SLOTS, FF), 1.0, 5.0, ((0, 16), (2, 2))),
        "w_gate": centred(splits[5], (EXPERTS, D, FF), (FF // 16) ** -0.5, 0.75, ((0, 16), (2, 2))),
        "w_up": centred(splits[6], (EXPERTS, D, FF), (FF // 16) ** -0.5, 0.75, ((0, 16), (2, 2))),
        "w_down": centred(splits[7], (EXPERTS, FF, D), (D * 64) ** -0.5, 0.0078125, ((0, 16), (1, 2))),
    }


def silu_parts(value):
    sigma = jax.nn.sigmoid(value)
    return value * sigma, sigma * (1.0 + value * (1.0 - sigma))


def pair_tables(group_ids):
    pair_count = group_ids.shape[0]
    fanout = group_ids.shape[1]
    assigned = group_ids.reshape(-1).astype(jnp.int32)
    one_hot = (assigned[:, None] == jnp.arange(EXPERTS, dtype=jnp.int32)[None, :]).astype(jnp.int32)
    earlier = jnp.cumsum(one_hot, axis=0) - one_hot
    position = jnp.sum(earlier * one_hot, axis=1).astype(jnp.int32)
    retained = (assigned < EXPERTS) & (position < CAP)
    slot_index = jnp.where(retained, assigned * CAP + position, EXPERTS * CAP).astype(jnp.int32)
    owner_row = (jnp.arange(assigned.shape[0], dtype=jnp.int32) // fanout).astype(jnp.int32)
    slot_rows = jnp.full((EXPERTS * CAP + 1,), pair_count, jnp.int32).at[slot_index].set(owner_row)
    return slot_index.reshape(pair_count, fanout), slot_rows[:EXPERTS * CAP].reshape(EXPERTS, CAP)


def reference(out_grad, route_ids, route_weights, gate_pre, up_pre, w_gate, w_up, w_down):
    pair_count = TOK_DEV * N_SEQ
    half_width = FF // N_SEQ
    grouped = route_ids.reshape(N_EXPERT, pair_count, TOPK)
    slot_index, slot_rows = jax.vmap(pair_tables)(grouped)
    offsets = (jnp.arange(N_EXPERT, dtype=jnp.int32) * pair_count)[:, None, None]
    global_rows = jnp.where(slot_rows == pair_count, TOKENS, slot_rows + offsets).astype(jnp.int32)
    expert_rows = jnp.transpose(global_rows, (1, 0, 2)).reshape(EXPERTS, SLOTS)
    padded_grad = jnp.concatenate([out_grad, jnp.zeros((1, D), jnp.bfloat16)], axis=0)

    def expert_work(inputs):
        rows, gate_val, up_val, gate_w, up_w, down_w = inputs
        slot_grad = padded_grad[rows]
        input_sum = jnp.zeros((SLOTS, D), jnp.float32)
        score_sum = jnp.zeros((SLOTS,), jnp.float32)
        for half_at in range(N_SEQ):
            lower = half_at * half_width
            upper = lower + half_width
            hidden_grad = jnp.dot(slot_grad, down_w[lower:upper].T, preferred_element_type=jnp.float32)
            active, slope_val = silu_parts(gate_val[:, lower:upper].astype(jnp.float32))
            up_part = up_val[:, lower:upper].astype(jnp.float32)
            score_part = jnp.sum(hidden_grad * active * up_part, axis=1)
            gate_diff = (hidden_grad * up_part * slope_val).astype(jnp.bfloat16)
            up_diff = (hidden_grad * active).astype(jnp.bfloat16)
            input_part = jnp.dot(gate_diff, gate_w[:, lower:upper].T, preferred_element_type=jnp.float32)
            input_part = input_part + jnp.dot(up_diff, up_w[:, lower:upper].T, preferred_element_type=jnp.float32)
            input_round = lax.optimization_barrier(input_part.astype(jnp.bfloat16))
            score_round = lax.optimization_barrier(score_part.astype(jnp.bfloat16))
            input_sum = input_sum + input_round.astype(jnp.float32)
            score_sum = score_sum + score_round.astype(jnp.float32)
        return input_sum.astype(jnp.bfloat16), score_sum.astype(jnp.bfloat16)

    slot_input, slot_score = lax.map(expert_work, (expert_rows, gate_pre, up_pre, w_gate, w_up, w_down))
    expert_of = slot_index // CAP
    place = slot_index % CAP
    group_of = jnp.arange(N_EXPERT, dtype=jnp.int32)[:, None, None]
    global_slot = jnp.where(slot_index == EXPERTS * CAP, EXPERTS * SLOTS, expert_of * SLOTS + group_of * CAP + place)
    global_slot = global_slot.astype(jnp.int32).reshape(TOKENS, TOPK)
    flat_input = jnp.concatenate([slot_input.reshape(EXPERTS * SLOTS, D), jnp.zeros((1, D), jnp.bfloat16)], axis=0)
    flat_score = jnp.concatenate([slot_score.reshape(EXPERTS * SLOTS), jnp.zeros((1,), jnp.bfloat16)], axis=0)
    in_grad = jnp.zeros((TOKENS, D), jnp.float32)
    for column in range(TOPK):
        in_grad = in_grad + route_weights[:, column:column + 1] * flat_input[global_slot[:, column]].astype(jnp.float32)
    return in_grad.astype(jnp.bfloat16), flat_score[global_slot]
```

```python
import jax
import jax.numpy as jnp
from jax import lax
from jax.sharding import PartitionSpec as P

BF = jnp.bfloat16
F32 = jnp.float32
NT = (((1,), (1,)), ((), ()))
NN = (((1,), (0,)), ((), ()))
TN = (((0,), (0,)), ((), ()))


def silu_parts(value):
    sigma = jax.nn.sigmoid(value)
    return (value * sigma, sigma * (1.0 + value * (1.0 - sigma)))


def dot(a, b, dims):
    return lax.dot_general(a, b, dims, preferred_element_type=F32)


def swap(value):
    return lax.ppermute(value, "seq", [(0, 1), (1, 0)])


def ordered(mine, theirs, seq_at, axis):
    low = jnp.where(seq_at == 0, mine, theirs)
    high = jnp.where(seq_at == 0, theirs, mine)
    return jnp.concatenate([low, high], axis=axis)


def routing(ids, weights, experts, capacity):
    tokens = ids.shape[0]
    same = ids[:, :, None] == jnp.arange(experts, dtype=jnp.int32)
    hit = jnp.any(same, axis=1)
    weight = jnp.sum(jnp.where(same, weights[:, :, None], 0.0), axis=1)
    row = jnp.arange(tokens, dtype=jnp.int32)
    earlier = (row[None, :] < row[:, None]).astype(BF)
    position = dot(earlier, hit.astype(BF), NN)
    slot = jnp.where(hit, position, float(capacity))
    return slot, weight


def on_device_xla(out_grad, route_ids, route_weights, gate_pre, up_pre, w_gate, w_up, w_down):
    n_expert = lax.axis_size("expert")
    seq_at = lax.axis_index("seq")
    own, width = out_grad.shape
    half = width // 2
    experts = n_expert
    slots = gate_pre.shape[1]
    capacity = slots // n_expert
    slot, weight = routing(route_ids, route_weights, experts, capacity)
    table = (slot[:, :, None] == jnp.arange(capacity, dtype=F32)).reshape(2 * own, slots)
    w_all = jnp.broadcast_to(weight[:, :, None], (2 * own, experts, capacity)).reshape(2 * own, slots)
    w_all = jnp.where(table, w_all, 0.0)
    w_hi = w_all.astype(BF)
    w_lo = (w_all - w_hi.astype(F32)).astype(BF)
    mine = lax.dynamic_slice_in_dim(out_grad, seq_at * half, half, 1)
    other = lax.dynamic_slice_in_dim(out_grad, (1 - seq_at) * half, half, 1)
    tokens = ordered(mine, swap(other), seq_at, 0)
    outgoing = dot(table.astype(BF), tokens, TN).astype(BF).reshape(experts, capacity, half)
    received = lax.all_to_all(outgoing, "expert", split_axis=0, concat_axis=0, tiled=True)
    received = received.reshape(slots, half)
    slot_grad = ordered(received, swap(received), seq_at, 1)
    hidden_grad = dot(slot_grad, w_down[0], NT)
    active, slope = silu_parts(gate_pre[0].astype(F32))
    up_part = up_pre[0].astype(F32)
    score = jnp.sum(hidden_grad * active * up_part, axis=1).astype(BF)
    gate_diff = (hidden_grad * up_part * slope).astype(BF)
    up_diff = (hidden_grad * active).astype(BF)
    part = (dot(gate_diff, w_gate[0], NT) + dot(up_diff, w_up[0], NT)).astype(BF)
    score = lax.optimization_barrier(score)
    part = lax.optimization_barrier(part)
    keep = lax.dynamic_slice_in_dim(part, seq_at * half, half, 1)
    give = lax.dynamic_slice_in_dim(part, (1 - seq_at) * half, half, 1)
    total = (keep.astype(F32) + swap(give).astype(F32)).astype(BF)
    total_score = (score.astype(F32) + swap(score).astype(F32)).astype(BF)
    back = lax.all_to_all(
        total.reshape(n_expert, capacity, half), "expert", split_axis=0, concat_axis=0, tiled=True
    ).reshape(slots, half)
    back_score = lax.all_to_all(
        total_score.reshape(n_expert, capacity), "expert", split_axis=0, concat_axis=0, tiled=True
    ).reshape(slots)
    rows = (dot(w_hi, back, NN) + dot(w_lo, back, NN)).astype(BF)
    keep = lax.dynamic_slice_in_dim(rows, seq_at * own, own, 0)
    give = lax.dynamic_slice_in_dim(rows, (1 - seq_at) * own, own, 0)
    in_grad = ordered(keep, swap(give), seq_at, 1)
    own_table = lax.dynamic_slice_in_dim(table, seq_at * own, own, 0)
    own_ids = lax.dynamic_slice_in_dim(route_ids, seq_at * own, own, 0)
    of_expert = jnp.sum(
        jnp.where(own_table, back_score.astype(F32)[None, :], 0.0).reshape(own, experts, capacity),
        axis=2,
    )
    same = own_ids[:, :, None] == jnp.arange(experts, dtype=jnp.int32)
    weight_grad = jnp.sum(jnp.where(same, of_expert[:, None, :], 0.0), axis=2)
    return in_grad, weight_grad.astype(BF)


def solution(mesh):
    in_specs = (
        P(("expert", "seq"), None),
        P("expert", None),
        P("expert", None),
        P("expert", None, "seq"),
        P("expert", None, "seq"),
        P("expert", None, "seq"),
        P("expert", None, "seq"),
        P("expert", "seq", None),
    )
    out_specs = (P(("expert", "seq"), None), P(("expert", "seq"), None))
    return jax.shard_map(
        on_device_xla, mesh=mesh, in_specs=in_specs, out_specs=out_specs, check_vma=False
    )
```

```python
import functools

import jax
import jax.numpy as jnp
from jax import lax
from jax.experimental import pallas as pl
from jax.experimental.pallas import tpu as pltpu
from jax.sharding import PartitionSpec as P

BF = jnp.bfloat16
F32 = jnp.float32
NT = (((1,), (1,)), ((), ()))
NN = (((1,), (0,)), ((), ()))
TN = (((0,), (0,)), ((), ()))


def silu_parts(value):
    sigma = jax.nn.sigmoid(value)
    return (value * sigma, sigma * (1.0 + value * (1.0 - sigma)))


def dot(a, b, dims):
    return lax.dot_general(a, b, dims, preferred_element_type=F32)


def swap(value):
    return lax.ppermute(value, "seq", [(0, 1), (1, 0)])


def ordered(mine, theirs, seq_at, axis):
    low = jnp.where(seq_at == 0, mine, theirs)
    high = jnp.where(seq_at == 0, theirs, mine)
    return jnp.concatenate([low, high], axis=axis)


def routing(ids, weights, experts, capacity):
    tokens = ids.shape[0]
    same = ids[:, :, None] == jnp.arange(experts, dtype=jnp.int32)
    hit = jnp.any(same, axis=1)
    weight = jnp.sum(jnp.where(same, weights[:, :, None], 0.0), axis=1)
    row = jnp.arange(tokens, dtype=jnp.int32)
    earlier = (row[None, :] < row[:, None]).astype(BF)
    position = dot(earlier, hit.astype(BF), NN)
    slot = jnp.where(hit, position, float(capacity))
    return slot, weight


def on_device_xla(out_grad, route_ids, route_weights, gate_pre, up_pre, w_gate, w_up, w_down):
    n_expert = lax.axis_size("expert")
    seq_at = lax.axis_index("seq")
    own, width = out_grad.shape
    half = width // 2
    experts = n_expert
    slots = gate_pre.shape[1]
    capacity = slots // n_expert
    slot, weight = routing(route_ids, route_weights, experts, capacity)
    table = (slot[:, :, None] == jnp.arange(capacity, dtype=F32)).reshape(2 * own, slots)
    w_all = jnp.broadcast_to(weight[:, :, None], (2 * own, experts, capacity)).reshape(2 * own, slots)
    w_all = jnp.where(table, w_all, 0.0)
    w_hi = w_all.astype(BF)
    w_lo = (w_all - w_hi.astype(F32)).astype(BF)
    mine = lax.dynamic_slice_in_dim(out_grad, seq_at * half, half, 1)
    other = lax.dynamic_slice_in_dim(out_grad, (1 - seq_at) * half, half, 1)
    tokens = ordered(mine, swap(other), seq_at, 0)
    outgoing = dot(table.astype(BF), tokens, TN).astype(BF).reshape(experts, capacity, half)
    received = lax.all_to_all(outgoing, "expert", split_axis=0, concat_axis=0, tiled=True)
    received = received.reshape(slots, half)
    slot_grad = ordered(received, swap(received), seq_at, 1)
    hidden_grad = dot(slot_grad, w_down[0], NT)
    active, slope = silu_parts(gate_pre[0].astype(F32))
    up_part = up_pre[0].astype(F32)
    score = jnp.sum(hidden_grad * active * up_part, axis=1).astype(BF)
    gate_diff = (hidden_grad * up_part * slope).astype(BF)
    up_diff = (hidden_grad * active).astype(BF)
    part = (dot(gate_diff, w_gate[0], NT) + dot(up_diff, w_up[0], NT)).astype(BF)
    score = lax.optimization_barrier(score)
    part = lax.optimization_barrier(part)
    keep = lax.dynamic_slice_in_dim(part, seq_at * half, half, 1)
    give = lax.dynamic_slice_in_dim(part, (1 - seq_at) * half, half, 1)
    total = (keep.astype(F32) + swap(give).astype(F32)).astype(BF)
    total_score = (score.astype(F32) + swap(score).astype(F32)).astype(BF)
    back = lax.all_to_all(
        total.reshape(n_expert, capacity, half), "expert", split_axis=0, concat_axis=0, tiled=True
    ).reshape(slots, half)
    back_score = lax.all_to_all(
        total_score.reshape(n_expert, capacity), "expert", split_axis=0, concat_axis=0, tiled=True
    ).reshape(slots)
    rows = (dot(w_hi, back, NN) + dot(w_lo, back, NN)).astype(BF)
    keep = lax.dynamic_slice_in_dim(rows, seq_at * own, own, 0)
    give = lax.dynamic_slice_in_dim(rows, (1 - seq_at) * own, own, 0)
    in_grad = ordered(keep, swap(give), seq_at, 1)
    own_table = lax.dynamic_slice_in_dim(table, seq_at * own, own, 0)
    own_ids = lax.dynamic_slice_in_dim(route_ids, seq_at * own, own, 0)
    of_expert = jnp.sum(
        jnp.where(own_table, back_score.astype(F32)[None, :], 0.0).reshape(own, experts, capacity),
        axis=2,
    )
    same = own_ids[:, :, None] == jnp.arange(experts, dtype=jnp.int32)
    weight_grad = jnp.sum(jnp.where(same, of_expert[:, None, :], 0.0), axis=2)
    return in_grad, weight_grad.astype(BF)


MESH = pl.DeviceIdType.MESH
PARTS = 4


def lanes(shape, axis):
    return lax.broadcasted_iota(jnp.int32, shape, axis).astype(F32)


def fdiv(value, by):
    return jnp.floor((value + 0.5) * (1.0 / by))


def ones(mask):
    return jnp.where(mask, 1.0, 0.0).astype(BF)


def step_kernel(
    n, cap, og, ids_ref, wt_ref, gp_ref, up_ref, wg_hbm, wu_hbm, wd_hbm,
    out_ref, wgrad_ref,
    wg, wu, wd, tok, snd, rxo, rxp, xo, xp, hid, gd, ud, pout, pin, ybuf, rx2, z,
    vbuf, whi, wlo, scs, sci, sco, scr, osend,
    s_tok, r_tok, l_tok, l_w, s_d, r_d, s_f, r_f, s_p, r_p, s_s, r_s, s_b, r_b, s_c, r_c,
    s_o, r_o, l_o,
):
    me = lax.axis_index("expert")
    s = lax.axis_index("seq")
    o = 1 - s
    own, width = og.shape
    half = width // 2
    slots = n * cap
    blk = PARTS * cap
    grp = PARTS * blk
    rows = PARTS * cap
    qw = half // PARTS
    quads = n // PARTS
    zat = me // PARTS

    barrier = pltpu.get_barrier_semaphore()
    pl.semaphore_signal(barrier, inc=1, device_id=(me, o), device_id_type=MESH)

    def greet(i, c):
        pl.semaphore_signal(
            barrier, inc=1, device_id=(lax.rem(me + i, n), s), device_id_type=MESH
        )
        return c

    lax.fori_loop(1, n, greet, 0)

    base = pl.multiple_of(s * half, 128)
    obase = pl.multiple_of(o * half, 128)
    mine = pl.multiple_of(s * own, 16)
    theirs = pl.multiple_of(o * own, 16)

    local_tok = pltpu.make_async_copy(
        og.at[:, pl.ds(base, half)], tok.at[pl.ds(mine, own), :], l_tok
    )
    local_tok.start()
    pl.semaphore_wait(barrier, n)

    def remote(src, dst, ss, rs, dev):
        return pltpu.make_async_remote_copy(
            src_ref=src, dst_ref=dst, send_sem=ss, recv_sem=rs, device_id=dev, device_id_type=MESH
        )

    tok_copy = remote(
        og.at[:, pl.ds(obase, half)], tok.at[pl.ds(mine, own), :], s_tok, r_tok, (me, o)
    )
    tok_copy.start()
    loads = [
        pltpu.make_async_copy(wd_hbm, wd, l_w.at[0]),
        pltpu.make_async_copy(wg_hbm, wg, l_w.at[1]),
        pltpu.make_async_copy(wu_hbm, wu, l_w.at[2]),
    ]

    tokens = 2 * own
    ids = ids_ref[...]
    wts = wt_ref[...]
    e_lane = lax.broadcasted_iota(jnp.int32, (tokens, n), 1)
    hit = jnp.zeros((tokens, n), F32)
    wte = jnp.zeros((tokens, n), F32)
    for k in range(ids_ref.shape[1]):
        same = ids[:, k : k + 1] == e_lane
        hit = jnp.where(same, 1.0, hit)
        wte = jnp.where(same, wts[:, k : k + 1], wte)
    tri = ones(lanes((tokens, tokens), 1) < lanes((tokens, tokens), 0))
    pos = dot(tri, hit.astype(BF), NN)
    v = jnp.where((hit > 0.5) & (pos < cap - 0.5), pos, 255.0)
    vbuf[...] = v
    vb = v.astype(BF)
    c = lanes((tokens, slots), 1)
    place = c - cap * fdiv(c, cap)
    ec = lanes((n, slots), 1)
    expand = ones(fdiv(ec, cap) == lanes((n, slots), 0))
    taken = dot(vb, expand, NN) == place
    hi = wte.astype(BF)
    lo = (wte - hi.astype(F32)).astype(BF)
    whi[...] = jnp.where(taken, dot(hi, expand, NN), 0.0).astype(BF)
    wlo[...] = jnp.where(taken, dot(lo, expand, NN), 0.0).astype(BF)
    r0 = lanes((grp, grp), 0)
    a0 = fdiv(r0, blk)
    b0 = fdiv(r0 - a0 * blk, cap)
    p0 = r0 - a0 * blk - b0 * cap
    perm = ones(lanes((grp, grp), 1) == b0 * blk + a0 * cap + p0)

    local_tok.wait()
    tok_copy.wait_recv()

    def d_copy(dest):
        at = pl.multiple_of(dest * blk, 16)
        to = pl.multiple_of(me * blk, 16)
        return remote(
            snd.at[pl.ds(at, blk), :], rxo.at[pl.ds(to, blk), :], s_d.at[dest], r_d.at[me], (dest, s)
        )

    def d_wait(src):
        at = pl.multiple_of(src * blk, 16)
        return remote(
            snd.at[pl.ds(at, blk), :], rxo.at[pl.ds(at, blk), :], s_d.at[src], r_d.at[src], (src, s)
        )

    def f_copy(src):
        at = pl.multiple_of(src * blk, 16)
        return remote(
            rxo.at[pl.ds(at, blk), :], rxp.at[pl.ds(at, blk), :], s_f.at[src], r_f.at[src], (me, o)
        )

    def own_copy():
        at = pl.multiple_of(me * blk, 16)
        return remote(
            snd.at[pl.ds(at, blk), :], rxp.at[pl.ds(at, blk), :], s_f.at[me], r_f.at[me], (me, o)
        )

    def dispatch(i, carry):
        quad = lax.rem(zat + 1 + i, quads)
        rr = lanes((rows, n), 0)
        pick = ones(fdiv(rr, cap) + (quad * PARTS).astype(F32) == lanes((rows, n), 1))
        vt = dot(pick, vb, NT)
        rt = lanes((rows, tokens), 0)
        sel = ones(vt == rt - cap * fdiv(rt, cap))
        stacked = jnp.concatenate(
            [dot(sel, tok[:, q * qw : (q + 1) * qw], NN).astype(BF) for q in range(PARTS)], axis=0
        )
        snd[pl.ds(pl.multiple_of(quad * grp, 16), grp), :] = dot(perm, stacked, NN).astype(BF)
        for j in range(PARTS):
            dest = quad * PARTS + j

            @pl.when(dest != me)
            def _():
                d_copy(dest).start()

            @pl.when(dest == me)
            def _():
                at = pl.multiple_of(me * blk, 16)
                rxo[pl.ds(at, blk), :] = snd[pl.ds(at, blk), :]
                own_copy().start()

        return carry

    lax.fori_loop(0, quads, dispatch, 0)
    for load in loads:
        load.start()

    def unpack(src, dst, quad):
        got = dot(perm, src[pl.ds(pl.multiple_of(quad * grp, 16), grp), :], NN).astype(BF)
        for q in range(PARTS):
            dst[pl.ds(pl.multiple_of(quad * rows, 16), rows), q * qw : (q + 1) * qw] = got[
                q * rows : (q + 1) * rows
            ]

    def collect(i, carry):
        quad = lax.rem(zat + 2 * quads - 1 - i, quads)
        for j in range(PARTS):
            src = quad * PARTS + j

            @pl.when(src != me)
            def _():
                d_wait(src).wait_recv()
                f_copy(src).start()

        unpack(rxo, xo, quad)
        for j in range(PARTS):
            f_copy(quad * PARTS + j).wait_recv()
        unpack(rxp, xp, quad)
        return carry

    lax.fori_loop(0, quads, collect, 0)

    hid[...] = jnp.zeros_like(hid)
    loads[0].wait()
    kw = 512

    def hidden(i, carry):
        at = pl.multiple_of(i * kw, 128)
        hid[...] += dot(
            xo[:, pl.ds(at, kw)], wd[:, pl.ds(pl.multiple_of(base + i * kw, 128), kw)], NT
        ) + dot(xp[:, pl.ds(at, kw)], wd[:, pl.ds(pl.multiple_of(obase + i * kw, 128), kw)], NT)
        return carry

    lax.fori_loop(0, half // kw, hidden, 0)
    active, slope = silu_parts(gp_ref[...].astype(F32))
    up = up_ref[...].astype(F32)
    grad = hid[...]
    ud_v = grad * active
    gd[...] = (grad * up * slope).astype(BF)
    ud[...] = ud_v.astype(BF)
    score = jnp.sum(ud_v * up, axis=1, keepdims=True)
    scs[...] = jnp.broadcast_to(score, (slots, 128)).astype(BF)
    sc_copy = remote(scs, sci, s_s, r_s, (me, o))
    sc_copy.start()
    loads[1].wait()
    loads[2].wait()

    def part(q, start):
        at = pl.ds(pl.multiple_of(start + q * qw, 128), qw)
        return (dot(gd[...], wg[at, :], NT) + dot(ud[...], wu[at, :], NT)).astype(BF)

    def p_copy(q):
        return remote(pout.at[q], pin.at[q], s_p.at[q], r_p.at[q], (me, o))

    def give(q, carry):
        pout[q] = part(q, obase)
        p_copy(q).start()
        return carry

    lax.fori_loop(0, PARTS, give, 0)

    def keep(q, carry):
        value = part(q, base).astype(F32)
        p_copy(q).wait_recv()
        ybuf[q] = (value + pin[q].astype(F32)).astype(BF)
        return carry

    lax.fori_loop(0, PARTS, keep, 0)

    sc_copy.wait_recv()
    total = (scs[...].astype(F32) + sci[...].astype(F32)).astype(BF)
    sr = lanes((n * 16, slots), 0)
    se = fdiv(sr, 16)
    sp = sr - 16 * se
    spread = ones((lanes((n * 16, slots), 1) == se * cap + sp) & (sp < cap - 0.5))
    sco[...] = dot(spread, total, NN).astype(BF)

    def wait_d(i, carry):
        d_copy(lax.rem(me + i, n)).wait_send()
        f_copy(lax.rem(me + i, n)).wait_send()
        return carry

    lax.fori_loop(1, n, wait_d, 0)
    own_copy().wait_send()

    def b_copy(dest):
        at = pl.multiple_of(dest * blk, 16)
        to = pl.multiple_of(me * blk, 16)
        return remote(
            snd.at[pl.ds(at, blk), :], rx2.at[pl.ds(to, blk), :], s_b.at[dest], r_b.at[me], (dest, s)
        )

    def b_wait(src):
        at = pl.multiple_of(src * blk, 16)
        return remote(
            snd.at[pl.ds(at, blk), :], rx2.at[pl.ds(at, blk), :], s_b.at[src], r_b.at[src], (src, s)
        )

    def c_copy(dest):
        at = pl.multiple_of(dest * 16, 16)
        to = pl.multiple_of(me * 16, 16)
        return remote(
            sco.at[pl.ds(at, 16), :], scr.at[pl.ds(to, 16), :], s_c.at[dest], r_c.at[me], (dest, s)
        )

    def c_wait(src):
        at = pl.multiple_of(src * 16, 16)
        return remote(
            sco.at[pl.ds(at, 16), :], scr.at[pl.ds(at, 16), :], s_c.at[src], r_c.at[src], (src, s)
        )

    def combine_send(i, carry):
        quad = lax.rem(zat + 1 + i, quads)
        at = pl.ds(pl.multiple_of(quad * rows, 16), rows)
        stacked = jnp.concatenate([ybuf[q, at, :] for q in range(PARTS)], axis=0)
        snd[pl.ds(pl.multiple_of(quad * grp, 16), grp), :] = dot(perm, stacked, NN).astype(BF)
        for j in range(PARTS):
            dest = quad * PARTS + j

            @pl.when(dest != me)
            def _():
                c_copy(dest).start()
                b_copy(dest).start()

            @pl.when(dest == me)
            def _():
                here = pl.ds(pl.multiple_of(me * blk, 16), blk)
                rx2[here, :] = snd[here, :]
                there = pl.ds(pl.multiple_of(me * 16, 16), 16)
                scr[there, :] = sco[there, :]

        return carry

    lax.fori_loop(0, quads, combine_send, 0)

    def collect2(i, carry):
        quad = lax.rem(zat + 2 * quads - 1 - i, quads)
        for j in range(PARTS):
            src = quad * PARTS + j

            @pl.when(src != me)
            def _():
                b_wait(src).wait_recv()
                c_wait(src).wait_recv()

        unpack(rx2, z, quad)
        return carry

    lax.fori_loop(0, quads, collect2, 0)

    def rows_of(start, q):
        zq = z[:, q * qw : (q + 1) * qw]
        at = pl.ds(start, own)
        return (dot(whi[at, :], zq, NN) + dot(wlo[at, :], zq, NN)).astype(BF)

    def o_copy(q):
        return remote(
            osend.at[q],
            out_ref.at[:, pl.ds(pl.multiple_of(base + q * qw, 128), qw)],
            s_o.at[q], r_o.at[q], (me, o),
        )

    def o_wait(q):
        return remote(
            osend.at[q],
            out_ref.at[:, pl.ds(pl.multiple_of(obase + q * qw, 128), qw)],
            s_o.at[q], r_o.at[q], (me, o),
        )

    def o_local(q):
        return pltpu.make_async_copy(
            osend.at[PARTS + q],
            out_ref.at[:, pl.ds(pl.multiple_of(base + q * qw, 128), qw)],
            l_o.at[q],
        )

    for q in range(PARTS):
        osend[q] = rows_of(theirs, q)
        o_copy(q).start()
    for q in range(PARTS):
        osend[PARTS + q] = rows_of(mine, q)
        o_local(q).start()

    vo = vbuf[pl.ds(mine, own), :].astype(BF)
    wide = n * 16
    wc = lanes((own, wide), 1)
    we = fdiv(wc, 16)
    spot = dot(vo, ones(fdiv(lanes((n, wide), 1), 16) == lanes((n, wide), 0)), NN) == wc - 16 * we
    ido = ids_ref[pl.ds(mine, own), :].astype(F32)
    acc = jnp.zeros((own, 128), F32)
    for k in range(ids_ref.shape[1]):
        sel = ones(spot & (we == ido[:, k : k + 1]))
        acc = jnp.where(lanes((own, 128), 1) == k, dot(sel, scr[...], NN), acc)
    wgrad_ref[...] = acc[:, : wgrad_ref.shape[1]].astype(BF)

    tok_copy.wait_send()
    sc_copy.wait_send()

    def drain(i, carry):
        dest = lax.rem(me + i, n)
        b_copy(dest).wait_send()
        c_copy(dest).wait_send()
        return carry

    lax.fori_loop(1, n, drain, 0)
    for q in range(PARTS):
        p_copy(q).wait_send()
        o_copy(q).wait_send()
        o_local(q).wait()
        o_wait(q).wait_recv()


def scratch(n, cap, own, width, hidden):
    half = width // 2
    slots = n * cap
    big = PARTS * slots
    qw = half // PARTS
    vm, dma = pltpu.VMEM, pltpu.SemaphoreType.DMA
    return [
        vm((width, hidden), BF), vm((width, hidden), BF), vm((hidden, width), BF),
        vm((2 * own, half), BF), vm((big, qw), BF), vm((big, qw), BF), vm((big, qw), BF),
        vm((slots, half), BF), vm((slots, half), BF), vm((slots, hidden), F32),
        vm((slots, hidden), BF), vm((slots, hidden), BF),
        vm((PARTS, slots, qw), BF), vm((PARTS, slots, qw), BF), vm((PARTS, slots, qw), BF),
        vm((big, qw), BF), vm((slots, half), BF),
        vm((2 * own, n), F32), vm((2 * own, slots), BF), vm((2 * own, slots), BF),
        vm((slots, 128), BF), vm((slots, 128), BF), vm((n * 16, 128), BF), vm((n * 16, 128), BF),
        vm((2 * PARTS, own, qw), BF),
        dma, dma, dma, dma((3,)),
        dma((n,)), dma((n,)), dma((n,)), dma((n,)), dma((PARTS,)), dma((PARTS,)), dma, dma,
        dma((n,)), dma((n,)), dma((n,)), dma((n,)), dma((PARTS,)), dma((PARTS,)), dma((PARTS,)),
    ]


def kernel_fits(n, cap, own, width, hidden):
    half = width // 2
    slots = n * cap
    size = 2 * (3 * width * hidden + 10 * slots * half + 4 * own * half)
    aligned = (PARTS * cap) % 16 == 0 and half % (PARTS * 128) == 0 and half % 512 == 0
    return n % PARTS == 0 and cap <= 16 and aligned and own % 16 == 0 and size < 48 * 2**20


def on_device(out_grad, route_ids, route_weights, gate_pre, up_pre, w_gate, w_up, w_down):
    n = lax.axis_size("expert")
    own, width = out_grad.shape
    slots, hidden = gate_pre.shape[1:]
    cap = slots // n
    args = (out_grad, route_ids, route_weights, gate_pre, up_pre, w_gate, w_up, w_down)
    if not kernel_fits(n, cap, own, width, hidden):
        return on_device_xla(*args)
    anywhere = pl.BlockSpec(memory_space=pl.ANY)
    vmem = pl.BlockSpec(memory_space=pltpu.VMEM)
    return pl.pallas_call(
        functools.partial(step_kernel, n, cap),
        out_shape=(
            jax.ShapeDtypeStruct((own, width), BF),
            jax.ShapeDtypeStruct((own, route_ids.shape[1]), BF),
        ),
        in_specs=[anywhere, vmem, vmem, vmem, vmem, anywhere, anywhere, anywhere],
        out_specs=(anywhere, vmem),
        scratch_shapes=scratch(n, cap, own, width, hidden),
        compiler_params=pltpu.CompilerParams(
            collective_id=0, has_side_effects=True, vmem_limit_bytes=63 * 2**20
        ),
        name="expert_step",
    )(
        out_grad, route_ids, route_weights, gate_pre[0], up_pre[0], w_gate[0], w_up[0], w_down[0]
    )


def solution(mesh):
    in_specs = (
        P(("expert", "seq"), None),
        P("expert", None),
        P("expert", None),
        P("expert", None, "seq"),
        P("expert", None, "seq"),
        P("expert", None, "seq"),
        P("expert", None, "seq"),
        P("expert", "seq", None),
    )
    out_specs = (P(("expert", "seq"), None), P(("expert", "seq"), None))
    return jax.shard_map(
        on_device, mesh=mesh, in_specs=in_specs, out_specs=out_specs, check_vma=False
    )
```
